128 devices in a mesh: seq: 32 (over z_hi, y, x), head: 4 (over z_lo, core).
Axes of the slice: x: 4, y: 4, z: 4 (z_hi: 2, z_lo: 2; z = z_hi * 2 + z_lo), core: 2. Of those that a mesh axis runs over, the one named last changes fastest.
Arguments:
- x_in: bfloat16 [16384, 4096], P('seq', 'head'), may hold values from -6 to 6
- z_in: bfloat16 [16384, 4096], P('seq', 'head'), may hold values from -6 to 6
- b_in: bfloat16 [16384, 512], P('seq', 'head'), may hold values from -0.5 to 0.5
- c_in: bfloat16 [16384, 512], P('seq', 'head'), may hold values from -0.5 to 0.5
- dt_raw: float32 [64, 16384], P('head', 'seq')
- dt_bias: float32 [64], P('head'), may hold values from -5 to -4
- a_log: float32 [64], P('head')
- d_skip: float32 [64], P('head'), may hold values from 0.1 to 1.9
- gain: float32 [4096], P('head'), may hold values from 0.5 to 1.5
- resets: int32 [64, 128], P('head', 'seq'), may hold values 0 or 1
- out_weight: bfloat16 [4096, 4096], P('seq', 'head'), may hold values from -0.09375 to 0.09375
- cotangent: bfloat16 [16384, 4096], P('seq', 'head'), may hold values from -6 to 6
Outputs:
- d_x: bfloat16 [16384, 4096], P('seq', 'head')
- d_z: bfloat16 [16384, 4096], P('seq', 'head')
- d_b: bfloat16 [16384, 512], P('seq', 'head')
- d_c: bfloat16 [16384, 512], P('seq', 'head')
- raw_timestep_gradient: float32 [64, 16384], P('head', 'seq')
- d_out_weight: float32 [4096, 4096], P('seq', 'head')
The draws below stay inside these ranges and needn't reach their ends.
All inputs are finite; a program needn't handle non-finite values. No bound on the sum of `resets` on one device may be relied on, other than what follows from the above.
Results may differ from the reference program's by a relative error of at most 0.0075.
Values may be sent and summed in bfloat16 or wider, within the bound.
A program may use at most 256 MiB of HBM per device.

```python
from functools import partial
import jax
import jax.numpy as jnp
from jax import lax

D = 4096
MIXER_HEADS = 64
HEADDIM = 64
STATE = 128
GROUPS = 4
BLOCK = 128
TOK_DEV = 512
INNER = 4096
SEQUENCE_LENGTH = 16384
NBLOCKS = 128


def draw_a_log(key, part):
    picker, levels = jax.random.split(jax.random.fold_in(key, 11))
    share = 0.5
    slow = jax.random.uniform(picker, (MIXER_HEADS,)) < share
    unit = jax.random.uniform(levels, (MIXER_HEADS,), dtype=jnp.float32)
    slow_value = jnp.log(40.0 / SEQUENCE_LENGTH) + unit * jnp.log(3.0)
    fast_value = jnp.log(1.5) + unit * jnp.log(2.0)
    return jnp.where(slow, slow_value, fast_value).astype(jnp.float32)


def draw_dt_raw(key, part):
    first, second, third_piece = jax.random.split(jax.random.fold_in(key, 23), 3)
    start_offsets = jax.random.uniform(first, (MIXER_HEADS, SEQUENCE_LENGTH // TOK_DEV, 1), minval=-0.7, maxval=0.7)
    start_offsets = jnp.broadcast_to(start_offsets, (MIXER_HEADS, SEQUENCE_LENGTH // TOK_DEV, TOK_DEV)).reshape(MIXER_HEADS, SEQUENCE_LENGTH)
    random_jitter = 0.4 * jax.random.normal(second, (MIXER_HEADS, SEQUENCE_LENGTH))
    document_runs = jax.random.uniform(third_piece, (MIXER_HEADS, SEQUENCE_LENGTH)) < 3.0 / SEQUENCE_LENGTH
    return (start_offsets + random_jitter + jnp.where(document_runs, 150.0, 0.0)).astype(jnp.float32)


def set_ends(drawn, stream_key, smallest, high):
    extent = drawn.shape
    index_at = [jax.random.randint(jax.random.fold_in(stream_key, axis), (), 0, extent[axis]) for axis in range(len(extent))]
    drawn = drawn.at[tuple(index_at)].set(smallest)
    longest = extent.index(max(extent))
    index_at[longest] = (index_at[longest] + 1) % extent[longest]
    return drawn.at[tuple(index_at)].set(high)


def raised(values, stream_key, source, target, shards_of, factor):
    owner, partner = [(jnp.arange(values.shape[dim]) // (values.shape[dim] // shards_of)).reshape([-1 if axis == dim else 1 for axis in range(values.ndim)]) for dim in (source, target)]
    chosen = jax.random.permutation(stream_key, shards_of)[partner]
    strong = (owner == chosen) | (owner == (partner + shards_of // 2) % shards_of)
    return jnp.where(strong, factor * values, values)


def shard_levels(rng, dims, cuts, low, largest):
    def one(dim, shards_of):
        heights = jax.random.uniform(jax.random.fold_in(jax.random.fold_in(rng, 6), dim), (shards_of,), jnp.float32, low / len(cuts), largest / len(cuts))
        return jnp.repeat(jnp.exp(heights), dims[dim] // shards_of).reshape((-1,) + (1,) * (len(dims) - dim - 1))

    factor_of = one(*cuts[0])
    for cut in cuts[1:]:
        factor_of = factor_of * one(*cut)
    return factor_of


def bell_draw(stream_key, shape, deviation, most, pieces=(), kind=jnp.bfloat16):
    loudness = shard_levels(stream_key, shape, pieces, -0.22, 0.18) if pieces else 1.0
    entries = jax.random.normal(stream_key, shape, jnp.float32) * deviation * loudness
    return jnp.minimum(jnp.maximum(entries, -most), most).astype(kind)


def heavy_noise(own_key, dims, scale, most, pieces, heavy, kind=jnp.bfloat16):
    array = scale * jax.random.normal(own_key, dims, jnp.float32)
    if pieces:
        array = array * shard_levels(own_key, dims, pieces, -0.22, 0.18)
    return jnp.clip(raised(array, jax.random.fold_in(own_key, 3), *heavy), -most, most).astype(kind)


def setup_inputs(seed: int = 0) -> dict:
    keys = jax.random.split(jax.random.key(seed), 13)
    x_in = bell_draw(keys[0], (SEQUENCE_LENGTH, INNER), 1.0, 6.0, ((0, 32), (1, 4)))
    z_in = bell_draw(keys[1], (SEQUENCE_LENGTH, INNER), 1.0, 6.0, ((0, 32), (1, 4)))
    b_in = bell_draw(keys[2], (SEQUENCE_LENGTH, GROUPS * STATE), STATE ** -0.5, 0.5, ((0, 32), (1, 4)))
    c_in = bell_draw(keys[3], (SEQUENCE_LENGTH, GROUPS * STATE), STATE ** -0.5, 0.5, ((0, 32), (1, 4)))
    dt_raw = draw_dt_raw(jax.random.fold_in(keys[12], 71), 0)
    dt_bias = jnp.clip(-5.0 + 1.0 * jax.random.uniform(keys[5], (MIXER_HEADS,), jnp.float32) ** shard_levels(keys[5], (MIXER_HEADS,), ((0, 4),), -0.2, 0.2), -5.0, -4.0)
    a_log = draw_a_log(jax.random.fold_in(keys[12], 71), 0)
    d_skip = jnp.clip(1.0 + 0.18 * jax.random.normal(keys[7], (MIXER_HEADS,), jnp.float32), 0.1, 1.9)
    gain = jnp.clip(1.0 + 0.1 * jax.random.normal(keys[8], (INNER,), jnp.float32), 0.5, 1.5)
    resets = set_ends((jax.random.randint(keys[9], (MIXER_HEADS, NBLOCKS), 0, 64) < 1).astype(jnp.int32), jax.random.fold_in(keys[9], 1), 0, 1)
    out_weight = bell_draw(keys[10], (D, INNER), INNER ** -0.5, 0.09375, ((0, 32), (1, 4)))
    cotangent = heavy_noise(keys[11], (SEQUENCE_LENGTH, D), 1.0, 6.0, ((0, 32), (1, 4)), (0, 1, 32, 2.75))
    return {"x_in": x_in, "z_in": z_in, "b_in": b_in, "c_in": c_in, "dt_raw": dt_raw, "dt_bias": dt_bias, "a_log": a_log, "d_skip": d_skip, "gain": gain, "resets": resets, "out_weight": out_weight, "cotangent": cotangent}


highest = lax.Precision.HIGHEST

def block_step(state, inputs, per_group, skip_gain):
    x_block, b_block, c_block, rate_block, step_block, keep_block = inputs
    running = jnp.cumsum(rate_block, axis=1)
    positions = rate_block.shape[1]
    lower = jnp.arange(positions)[:, None] >= jnp.arange(positions)[None, :]
    spread = jnp.where(lower[None], running[:, :, None] - running[:, None, :], 0.0)
    decays = jnp.exp(spread) * lower[None].astype(jnp.float32)
    scores = jnp.einsum('tgn,sgn->gts', c_block, b_block, precision=highest)
    scores = jnp.repeat(scores, per_group, axis=0)
    mixing = scores * decays * step_block[:, None, :]
    within = jnp.einsum('hts,shp->thp', mixing, x_block, precision=highest)
    c_heads = jnp.repeat(c_block, per_group, axis=1)
    b_heads = jnp.repeat(b_block, per_group, axis=1)
    carried = state * keep_block[:, None, None]
    incoming = jnp.einsum('thn,hpn->thp', c_heads, carried, precision=highest) * jnp.exp(running).T[:, :, None]
    output = within + incoming + skip_gain[None, :, None] * x_block
    weighted = (jnp.exp(running[:, -1:] - running) * step_block).T
    fresh = jnp.einsum('sh,shp,shn->hpn', weighted, x_block, b_heads, precision=highest)
    return (carried * jnp.exp(running[:, -1])[:, None, None] + fresh, output)

def scan_blocks(inputs, bmatrix, cmatrix, dt_raw, start, dt_bias, a_log, d_skip, keep):
    positions = inputs.shape[0]
    heads = dt_raw.shape[0]
    groups = bmatrix.shape[1] // STATE
    blocks = positions // BLOCK
    step_size = jax.nn.softplus(dt_raw + dt_bias[:, None])
    rate = -step_size * jnp.exp(a_log)[:, None]
    x_blocks = inputs.reshape(blocks, BLOCK, heads, HEADDIM)
    b_blocks = bmatrix.reshape(blocks, BLOCK, groups, STATE)
    c_blocks = cmatrix.reshape(blocks, BLOCK, groups, STATE)
    rate_blocks = rate.reshape(heads, blocks, BLOCK).transpose(1, 0, 2)
    step_blocks = step_size.reshape(heads, blocks, BLOCK).transpose(1, 0, 2)
    stepper = partial(block_step, per_group=heads // groups, skip_gain=d_skip)
    final, outputs = lax.scan(stepper, start, (x_blocks, b_blocks, c_blocks, rate_blocks, step_blocks, keep.T))
    return (outputs.reshape(positions, heads * HEADDIM), final)

def gate_norm(mixed, gates, gain, groups):
    gated = mixed * jax.nn.silu(gates)
    count = gated.shape[0]
    grouped = gated.reshape(count, groups, -1)
    factor = lax.rsqrt(lax.optimization_barrier(jnp.mean(grouped * grouped, axis=2, keepdims=True)) + 1e-05)
    return (grouped * factor).reshape(count, -1) * gain

def reference(x_in, z_in, b_in, c_in, dt_raw, dt_bias, a_log, d_skip, gain, resets, out_weight, cotangent):
    keep = 1.0 - resets.astype(jnp.float32)
    zero_state = jnp.zeros((MIXER_HEADS, HEADDIM, STATE), jnp.float32)

    def forward(x_wide, input_matrix_wide, c_wide, raw_steps, z_wide):
        mixed, final = scan_blocks(x_wide, input_matrix_wide, c_wide, raw_steps, zero_state, dt_bias, a_log, d_skip, keep)
        return gate_norm(mixed, z_wide, gain, GROUPS)
    normed, pullback = jax.vjp(forward, x_in.astype(jnp.float32), b_in.astype(jnp.float32), c_in.astype(jnp.float32), dt_raw, z_in.astype(jnp.float32))
    normed_half = normed.astype(jnp.bfloat16)
    d_normed = jnp.dot(cotangent, out_weight, preferred_element_type=jnp.float32)
    grad_x, grad_b, grad_c, grad_steps, grad_z = pullback(d_normed)
    d_out_weight = jnp.dot(cotangent.T, normed_half, preferred_element_type=jnp.float32)
    return (grad_x.astype(jnp.bfloat16), grad_z.astype(jnp.bfloat16), grad_b.astype(jnp.bfloat16), grad_c.astype(jnp.bfloat16), grad_steps, d_out_weight)
```

```python
import jax
import jax.numpy as jnp
from jax import lax
from jax.sharding import PartitionSpec as P

HEADDIM = 64
STATE = 128
BLOCK = 128


high = lax.Precision.HIGH
highest = lax.Precision.HIGHEST


def gate_norm(mixed, gates, gain, groups):
    gated = mixed * jax.nn.silu(gates)
    count = gated.shape[0]
    grouped = gated.reshape(count, groups, -1)
    factor = lax.rsqrt(jnp.mean(grouped * grouped, axis=2, keepdims=True) + 1e-05)
    return (grouped * factor).reshape(count, -1) * gain


def exchange(value):
    return lax.all_to_all(value, "seq", split_axis=1, concat_axis=0, tiled=False)


def give_back(value, shape):
    parts = lax.all_to_all(value, "seq", split_axis=0, concat_axis=1, tiled=False)
    return parts.reshape(shape)


def local_terms(x_value, b_value, c_value, raw_steps, dt_bias, a_log, d_skip):
    heads = raw_steps.shape[0]
    blocks = x_value.shape[0]
    step_size = jax.nn.softplus(raw_steps + dt_bias[:, None])
    rate = -step_size * jnp.exp(a_log)[:, None]
    rate = rate.reshape(heads, blocks, BLOCK)
    step_size = step_size.reshape(heads, blocks, BLOCK)
    running = jnp.cumsum(rate, axis=2)
    lower = jnp.arange(BLOCK)[:, None] >= jnp.arange(BLOCK)[None, :]
    spread = jnp.where(lower, running[:, :, :, None] - running[:, :, None, :], 0.0)
    decays = jnp.exp(spread) * lower.astype(jnp.float32)
    scores = jnp.einsum("ktn,ksn->kts", c_value, b_value, precision=high)
    mixing = scores[None] * decays * step_size[:, :, None, :]
    within = jnp.einsum("hkts,kshp->kthp", mixing, x_value, precision=high)
    local = within + d_skip[:, None] * x_value
    weighted = jnp.exp(running[:, :, -1:] - running) * step_size
    scaled = x_value * weighted.transpose(1, 2, 0)[:, :, :, None]
    fresh = jnp.einsum("kshp,ksn->khpn", scaled, b_value, precision=high)
    block_decay = jnp.exp(running[:, :, -1])
    from_start = jnp.exp(running).transpose(1, 2, 0)
    return local, fresh, block_decay, from_start


def chain(fresh, block_decay, keep, start):
    state = start
    entering = []
    for block in range(fresh.shape[0]):
        carried = state * keep[:, block, None, None]
        entering.append(carried)
        state = carried * block_decay[:, block, None, None] + fresh[block]
    return jnp.stack(entering), state


def from_states(c_value, carried, from_start):
    incoming = jnp.einsum("ktn,khpn->kthp", c_value, carried, precision=high)
    return incoming * from_start[:, :, :, None]


def body(
    x_in, z_in, b_in, c_in, dt_raw, dt_bias, a_log, d_skip, gain, resets, out_weight, cotangent
):
    heads = dt_raw.shape[0]
    groups = b_in.shape[1] // STATE
    positions = x_in.shape[0]
    blocks = positions // BLOCK
    count = lax.axis_size("seq")
    share = HEADDIM // count
    shape = (heads, HEADDIM, STATE)
    weight = lax.all_gather(out_weight, "seq", axis=0, tiled=True)
    gathered = lax.all_gather(cotangent, "head", axis=0, tiled=False)
    keep = 1.0 - resets.astype(jnp.float32)
    x_wide = x_in.astype(jnp.float32).reshape(blocks, BLOCK, heads, HEADDIM)
    b_wide = b_in.astype(jnp.float32).reshape(blocks, BLOCK, STATE)
    c_wide = c_in.astype(jnp.float32).reshape(blocks, BLOCK, STATE)
    z_wide = z_in.astype(jnp.float32)

    def local_part(x_value, b_value, c_value, raw_steps):
        return local_terms(x_value, b_value, c_value, raw_steps, dt_bias, a_log, d_skip)

    (local, fresh, block_decay, from_start), local_pull = jax.vjp(
        local_part, x_wide, b_wide, c_wide, dt_raw
    )
    own = chain(fresh, block_decay, keep, jnp.zeros(shape, jnp.float32))[1]
    slab_decay = jnp.prod(block_decay * keep, axis=1)
    marks = jnp.broadcast_to(slab_decay[:, None, None, None], (heads, count, 1, STATE))
    outgoing = jnp.concatenate([own.reshape(heads, count, share, STATE), marks], axis=2)
    pieces = exchange(outgoing)
    slab_decays = pieces[:, :, share, 0]
    place = jnp.arange(count)
    between = (place[None, None, :] < place[:, None, None]) & (
        place[None, None, :] > place[None, :, None]
    )
    factors = jnp.where(between[None], slab_decays.T[:, None, None, :], 1.0)
    earlier = (place[None, :] < place[:, None]).astype(jnp.float32)
    paths = jnp.prod(factors, axis=3) * earlier[None]
    summed = jnp.einsum("hji,ihpn->jhpn", paths, pieces[:, :, :share], precision=highest)
    entering = give_back(summed, shape)

    def states(fresh_value, decay_value, start):
        return chain(fresh_value, decay_value, keep, start)

    (carried, leaving), states_pull = jax.vjp(states, fresh, block_decay, entering)
    incoming, incoming_pull = jax.vjp(from_states, c_wide, carried, from_start)
    mixed = (local + incoming).reshape(positions, heads * HEADDIM)

    def norming(mixed_value, z_value):
        return gate_norm(mixed_value, z_value, gain, groups)

    normed, norm_pull = jax.vjp(norming, mixed, z_wide)
    normed_half = normed.astype(jnp.bfloat16)
    owners = gathered.shape[0]
    d_out_weight = lax.psum_scatter(
        jnp.einsum("gtd,ti->gdi", gathered, normed_half, preferred_element_type=jnp.float32)
        .reshape(out_weight.shape[0] * count, normed_half.shape[1]),
        "seq",
        scatter_dimension=0,
        tiled=True,
    )
    d_normed = jnp.einsum(
        "gtd,gdi->ti",
        gathered,
        weight.reshape(owners, -1, weight.shape[1]),
        preferred_element_type=jnp.float32,
    )
    d_mixed, grad_z = norm_pull(d_normed)
    d_local = d_mixed.reshape(blocks, BLOCK, heads, HEADDIM)
    grad_c_states, d_carried, d_from_start = incoming_pull(d_local)
    start_grad = states_pull((d_carried, jnp.zeros(shape, jnp.float32)))[2]
    back_pieces = exchange(start_grad.reshape(heads, count, share, STATE))
    back_summed = jnp.einsum("hij,ihpn->jhpn", paths, back_pieces, precision=highest)
    arriving = give_back(back_summed, shape)
    d_fresh, d_block_decay, unused = states_pull((d_carried, arriving))
    grad_x, grad_b, grad_c, grad_steps = local_pull(
        (d_local, d_fresh, d_block_decay, d_from_start)
    )
    grad_c = grad_c + grad_c_states
    return (
        grad_x.reshape(positions, heads * HEADDIM).astype(jnp.bfloat16),
        grad_z.astype(jnp.bfloat16),
        grad_b.reshape(positions, STATE).astype(jnp.bfloat16),
        grad_c.reshape(positions, STATE).astype(jnp.bfloat16),
        grad_steps,
        d_out_weight,
    )


def solution(mesh):
    return jax.shard_map(
        body,
        mesh=mesh,
        in_specs=(
            P("seq", "head"),
            P("seq", "head"),
            P("seq", "head"),
            P("seq", "head"),
            P("head", "seq"),
            P("head"),
            P("head"),
            P("head"),
            P("head"),
            P("head", "seq"),
            P("seq", "head"),
            P("seq", "head"),
        ),
        out_specs=(
            P("seq", "head"),
            P("seq", "head"),
            P("seq", "head"),
            P("seq", "head"),
            P("head", "seq"),
            P("seq", "head"),
        ),
        check_vma=False,
    )
```
